32 devices in a mesh: groups: 2 (over y), feat: 4 (over z), rows: 2 (over x), sub: 2 (over core).
Axes of the slice: x: 2, y: 2, z: 4, core: 2. Of those that a mesh axis runs over, the one named last changes fastest.
Arguments:
- activations: bfloat16 [8192, 28672], P(('groups', 'rows', 'sub'), 'feat'), parts along dimension 0, may hold values from -6 to 6
- out_grads: bfloat16 [8192, 8192], P(('groups', 'rows', 'sub'), 'feat'), parts along dimension 0, may hold values from -6 to 6
- proj_in: bfloat16 [57344, 128], P(('groups', 'feat')), parts along dimension 0, may hold values from -0.03125 to 0.03125
- proj_out: bfloat16 [16384, 128], P(('groups', 'feat')), parts along dimension 0, may hold values from -0.0625 to 0.0625
- lengths: int32 [256], P('groups'), parts along dimension 0, may hold values from 1 to 64, 4096 in all
- corpus: bfloat16 [16384, 16384], P(('groups', 'rows', 'sub'), 'feat'), parts along dimension 0, may hold values from -200 to 200
- owner: int32 [8192], P(('rows', 'sub')), may hold values from 0 to 255, as said below
Outputs:
- influence: float32 [256, 16384], P(('groups', 'rows', 'sub'), 'feat'), parts along dimension 0
The draws below stay inside these ranges and needn't reach their ends.
There are 2 independent parts, one for each index of `groups`. The reference program is written for one: setup_inputs(seed, part) draws one part's arguments, and reference() takes and returns one part's arrays. A program takes and returns all parts, laid end to end along the dimension named above; an argument that names none is the same for every part. Nothing has to cross between parts.
Inputs may be any that keep to these rules, and one draw needn't show every extreme that they name: `owner`: every draw holds at least two different labels, so each passage keeps some corpus rows.
All inputs are finite; a program needn't handle non-finite values.
Results may differ from the reference program's by a relative error of at most 0.007.
The reference program's roundings to bfloat16 on the way count: a program that leaves them out, or rounds other values in their place, can miss the bound.
Values may be sent and summed in bfloat16 or wider, within the bound.
A program may use at most 128 MiB of HBM per device.

```python
import math
import jax
import jax.numpy as jnp
import numpy as np
from jax import lax

DIN = 28672
DOUT = 8192
RANK = 128
LONGEST = 64
K = 16384
P_SIZE = 128
TOK = 4096
R = 8192


def draw_corpus(key, part):
    first = jax.random.fold_in(jax.random.fold_in(key, 11), 0)
    base = jnp.clip(jax.random.normal(first, (R, K), jnp.float32), -6.0, 6.0)
    return base.astype(jnp.bfloat16)


def draw_owner(key, part):
    labels = jax.random.randint(jax.random.fold_in(key, 23), (R,), 0, 2 * P_SIZE).astype(jnp.int32)
    labels = labels.at[0].set(2 * P_SIZE - 1)
    labels = labels.at[R - 1].set(0)
    return labels


def level_of(rng, shape, shards, least, top_value):
    loudness, own = 1.0, jax.random.fold_in(rng, 6)
    for position, blocks in shards:
        draws = jnp.exp(jax.random.uniform(jax.random.fold_in(own, position), (blocks,), jnp.float32, least / len(shards), top_value / len(shards)))
        loudness = loudness * jnp.repeat(draws, shape[position] // blocks).reshape([-1 if axis == position else 1 for axis in range(len(shape))])
    return loudness


def length_profile(count, total, most, slope):
    portions = [(1 << 20) // math.isqrt(grade ** slope) + 1 for grade in range(2, count + 1)]
    rest, counts = total - most - (count - 1), [1] * (count - 1)
    while rest > 0:
        candidates = [i for i in range(count - 1) if counts[i] < most]
        mass, budget = sum([portions[i] for i in candidates]), rest
        for i in candidates:
            extra = min(most - counts[i], max(1, budget * portions[i] // mass), rest)
            counts[i] = counts[i] + extra
            rest = rest - extra
    return np.array([most] + counts)


def ragged(stream_key, amount, total, reach, slope):
    if amount == 2:
        one = jax.random.randint(stream_key, (), max(1, total - reach), min(reach, total - 1) + 1)
        return jnp.stack([one, total - one])
    sizes = jnp.asarray(length_profile(amount, total, reach, slope), jnp.int32)
    couples = (amount - 1) // 2
    source_of, receiver = sizes[1:1 + 2 * couples:2], sizes[2:2 + 2 * couples:2]
    slack = jnp.minimum(source_of - 1, reach - receiver)
    passed = jax.random.randint(jax.random.fold_in(stream_key, 1), (couples,), 0, 1 << 20) % (slack + 1)
    sizes = sizes.at[1:1 + 2 * couples:2].set(source_of - passed).at[2:2 + 2 * couples:2].set(receiver + passed)
    return sizes[jax.random.permutation(jax.random.fold_in(stream_key, 2), amount)]


def noise(key, extent, deviation, most, pieces=(), kind=jnp.bfloat16):
    factor_of = level_of(key, extent, pieces, -0.22, 0.18) if pieces else 1.0
    entries = jax.random.normal(key, extent, jnp.float32) * deviation * factor_of
    return jnp.minimum(jnp.maximum(entries, -most), most).astype(kind)


def setup_inputs(seed: int = 0, part: int = 0) -> dict:
    seeds = jax.random.split(jax.random.key(seed), 8)
    part_keys = jax.random.split(jax.random.fold_in(seeds[7], part), 8)
    return {
        "activations": noise(part_keys[0], (TOK, DIN), 1.0, 6.0, ((0, 4), (1, 4))),
        "out_grads": noise(part_keys[1], (TOK, DOUT), 1.0, 6.0, ((0, 4), (1, 4))),
        "proj_in": noise(part_keys[2], (DIN, RANK), DIN ** -0.5, 0.03125, ((0, 4),)),
        "proj_out": noise(part_keys[3], (DOUT, RANK), DOUT ** -0.5, 0.0625, ((0, 4),)),
        "lengths": ragged(part_keys[4], P_SIZE, TOK, LONGEST, 0).astype(jnp.int32),
        "corpus": draw_corpus(jax.random.fold_in(jax.random.fold_in(seeds[7], part), 71), part),
        "owner": draw_owner(jax.random.fold_in(seeds[7], 71), part),
    }


def reference(activations, out_grads, proj_in, proj_out, lengths, corpus, owner):
    x_low = jnp.dot(activations, proj_in, preferred_element_type=jnp.float32).astype(jnp.bfloat16)
    g_low = jnp.dot(out_grads, proj_out, preferred_element_type=jnp.float32).astype(jnp.bfloat16)
    ends = jnp.cumsum(lengths).astype(jnp.int32)
    starts = (ends - lengths).astype(jnp.int32)
    positions = jnp.arange(TOK, dtype=jnp.int32)
    member = ((positions[None, :] >= starts[:, None]) & (positions[None, :] < ends[:, None])).astype(jnp.bfloat16)

    def one_column(column):
        return jnp.dot(member * column[None, :], x_low, preferred_element_type=jnp.float32)
    stacked = lax.map(one_column, jnp.transpose(g_low))
    pgrad = jnp.transpose(stacked, (1, 0, 2)).reshape(P_SIZE, K)
    sumsq = lax.optimization_barrier(jnp.sum(pgrad * pgrad, axis=1))
    scale = 2.5 / math.sqrt(K) * lax.rsqrt(sumsq / K + 1e-06)
    raw = lax.dot_general(pgrad.astype(jnp.bfloat16), corpus, (((1,), (1,)), ((), ())), preferred_element_type=jnp.float32)
    score = raw * scale[:, None]
    owned = owner[None, :] == jnp.arange(P_SIZE, dtype=jnp.int32)[:, None]
    top = lax.optimization_barrier(jnp.max(jnp.where(owned, jnp.float32(-1e+30), score), axis=1))
    weight = jnp.where(owned, jnp.float32(0.0), jnp.exp(score - top[:, None]))
    total = lax.optimization_barrier(jnp.sum(weight, axis=1))
    summed = jnp.dot(weight.astype(jnp.bfloat16), corpus, preferred_element_type=jnp.float32)
    return summed / total[:, None]
```

```python
import functools
import math

import jax
import jax.numpy as jnp
from jax import lax
from jax.experimental import pallas as pl
from jax.experimental.pallas import tpu as pltpu
from jax.sharding import PartitionSpec as P

MESH = pl.DeviceIdType.MESH
F32 = jnp.float32
BF16 = jnp.bfloat16
NT = (((1,), (1,)), ((), ()))
WINDOW = 256


def remote(src, dst, send, recv, target):
    return pltpu.make_async_remote_copy(
        src_ref=src, dst_ref=dst, send_sem=send, recv_sem=recv,
        device_id=target, device_id_type=MESH)


def kernel(nz, nx, ns, win, act, og, pin, pout, owner, corpus, out,
           act_v, og_v, pin_v, pout_v, cor_v,
           g_send, g_recv, x_send, x_recv, x_all, gt_all, x_blk, g_blk, pgf, pg_low, sq,
           raw_send, raw_recv, w_all, st_x, st_s, fac,
           dbuf, dpart, d2, d3,
           ld, ldc, gs, gr, xs, xr, xzs, xzr, gis, gir, xis, xir, fws, fwr,
           rs, rr, ws, wr, fs, fr, sxs, sxr, sss, ssr, d1s, d1r, d2s, d2r):
    mz, mx, ms = lax.axis_index("feat"), lax.axis_index("rows"), lax.axis_index("sub")
    tok, _ = act.shape
    ni = nx * ns
    total_tok = tok * ni
    passages = win.shape[1]
    rank = pin.shape[1]
    cols = rank // nz
    tc = tok // nz
    rows, kc = corpus.shape
    pcz = passages // nz
    pci = passages // ni
    nb, rb = raw_send.shape[0], raw_send.shape[3] - 128
    ncb, cb = dbuf.shape[0], dbuf.shape[3]
    k_total = rank * rank
    os = lax.rem(ms + 1, ns)
    mi = mx * ns + ms

    def zp(o):
        return lax.rem(mz + o, nz)

    def xp(o):
        return lax.rem(mx + o, nx)

    c_og = pltpu.make_async_copy(og, og_v, ld.at[0])
    c_po = pltpu.make_async_copy(pout, pout_v, ld.at[1])
    c_pi = pltpu.make_async_copy(pin, pin_v, ld.at[2])
    c_po.start()
    c_og.start()
    c_pi.start()
    c_act = []
    for o in range(1, nz + 1):
        d = zp(o)
        at = pl.ds(pl.multiple_of(d * tc, tc), tc)
        c_act.append(pltpu.make_async_copy(act.at[at], act_v.at[at], ld.at[2 + o]))
        c_act[-1].start()
    c_cor = []
    for b in range(nb):
        at = pl.ds(b * rb, rb)
        c_cor.append(pltpu.make_async_copy(corpus.at[at], cor_v.at[at], ldc.at[b]))

    barrier = pltpu.get_barrier_semaphore()
    for o in range(1, nz):
        pl.semaphore_signal(barrier, inc=1, device_id={"feat": zp(o)}, device_id_type=MESH)
    for o in range(1, nx):
        pl.semaphore_signal(barrier, inc=1, device_id={"rows": xp(o)}, device_id_type=MESH)
    pl.semaphore_signal(barrier, inc=1, device_id={"sub": os}, device_id_type=MESH)
    pl.semaphore_wait(barrier, nz - 1 + nx - 1 + 1)

    c_po.wait()
    c_og.wait()
    g_t = jnp.transpose(jnp.dot(og_v[...], pout_v[...], preferred_element_type=F32))
    for j in range(nz):
        g_send[j] = g_t[j * cols:(j + 1) * cols]
    g_copies = [remote(g_send.at[zp(o)], g_recv.at[mz], gs.at[o - 1], gr.at[mz], {"feat": zp(o)})
                for o in range(1, nz)]
    for c in g_copies:
        c.start()

    c_pi.wait()
    x_copies = []
    for o in range(1, nz + 1):
        d = zp(o)
        at = pl.ds(pl.multiple_of(d * tc, tc), tc)
        c_act[o - 1].wait()
        x_send[d] = jnp.dot(act_v[at], pin_v[...], preferred_element_type=F32)
        if o < nz:
            c = remote(x_send.at[d], x_recv.at[mz], xs.at[o - 1], xr.at[mz], {"feat": d})
            c.start()
            x_copies.append(c)
        if o == max(1, nz // 2):
            for c in c_cor:
                c.start()

    def wait_recv(dst, sem, target):
        remote(dst, dst, sem, sem, target).wait_recv()

    g_sum = g_send[mz]
    for o in range(1, nz):
        s = zp(o)
        wait_recv(g_recv.at[s], gr.at[s], {"feat": s})
        g_sum = g_sum + g_recv[s]

    def tok_at(x, s):
        return pl.ds(pl.multiple_of((x * ns + s) * tok, tok), tok)

    mine = tok_at(mx, ms)
    gt_all[:, mine] = g_sum.astype(BF16)
    gi = []
    for o in range(1, nx):
        gi.append(remote(gt_all.at[:, mine], gt_all.at[:, mine], gis.at[o - 1], gir.at[mx], {"rows": xp(o)}))
    gi.append(remote(gt_all.at[:, mine], gt_all.at[:, mine], gis.at[nx - 1], fwr.at[0, mx], {"sub": os}))
    for c in gi:
        c.start()

    x_sum = x_send[mz]
    for o in range(1, nz):
        s = zp(o)
        wait_recv(x_recv.at[s], xr.at[s], {"feat": s})
        x_sum = x_sum + x_recv[s]

    def chunk_at(z):
        return pl.ds(pl.multiple_of((mi * nz + z) * tc, tc), tc)

    own = chunk_at(mz)
    x_all[own] = x_sum.astype(BF16)
    xz = [remote(x_all.at[own], x_all.at[own], xzs.at[o - 1], xzr.at[mz], {"feat": zp(o)}) for o in range(1, nz)]
    for c in xz:
        c.start()

    fw = []
    for o in range(1, nx):
        s = xp(o)
        at = tok_at(s, ms)
        wait_recv(gt_all.at[:, at], gir.at[s], {"rows": s})
        c = remote(gt_all.at[:, at], gt_all.at[:, at], fws.at[0, o - 1], fwr.at[0, s], {"sub": os})
        c.start()
        fw.append(c)

    for o in range(1, nz):
        s = zp(o)
        wait_recv(x_all.at[chunk_at(s)], xzr.at[s], {"feat": s})

    xi = []
    for o in range(1, nx):
        xi.append(remote(x_all.at[mine], x_all.at[mine], xis.at[o - 1], xir.at[mx], {"rows": xp(o)}))
    xi.append(remote(x_all.at[mine], x_all.at[mine], xis.at[nx - 1], fwr.at[1, mx], {"sub": os}))
    for c in xi:
        c.start()
    for o in range(1, nx):
        s = xp(o)
        at = tok_at(s, ms)
        wait_recv(x_all.at[at], xir.at[s], {"rows": s})
        c = remote(x_all.at[at], x_all.at[at], fws.at[1, o - 1], fwr.at[1, s], {"sub": os})
        c.start()
        fw.append(c)
    for x in range(nx):
        at = tok_at(x, os)
        wait_recv(gt_all.at[:, at], fwr.at[0, x], {"sub": os})
        wait_recv(x_all.at[at], fwr.at[1, x], {"sub": os})

    for i in range(total_tok // 128):
        g_blk[i] = gt_all[:, i * 128:(i + 1) * 128].astype(F32)
        x_blk[i] = x_all[i * 128:(i + 1) * 128, :]
    lane = lax.broadcasted_iota(jnp.int32, (cols, WINDOW), 1)

    def passage(p, carry):
        keep = (lane >= win[1, p]) & (lane < win[2, p])
        first = win[0, p]
        second = win[3, p]
        gw = jnp.concatenate([g_blk[first], g_blk[second]], axis=1)
        gw = jnp.where(keep, gw, 0.0).astype(BF16)
        xw = jnp.concatenate([x_blk[first], x_blk[second]], axis=0)
        res = jnp.dot(gw, xw, preferred_element_type=F32)
        pgf[pl.ds(p, cols, stride=passages), :] = res
        sq[pl.ds(p, 1), :] = jnp.sum(res * res, axis=0, keepdims=True)
        return carry

    lax.fori_loop(0, passages, passage, 0, unroll=8)
    for a in range(cols):
        pg_low[:, a * rank:(a + 1) * rank] = pgf[a * passages:(a + 1) * passages, :].astype(BF16)
    sumsq = jnp.sum(sq[...], axis=1, keepdims=True) + jnp.zeros((passages, 128), F32)

    for b in range(nb):
        c_cor[b].wait()

    def score_block(b, carry):
        at = pl.ds(pl.multiple_of(b * rb, rb), rb)
        raw = lax.dot_general(pg_low[...], cor_v[at, :], NT, preferred_element_type=F32)
        for j in range(nz):
            raw_send[b, j, :, :rb] = raw[j * pcz:(j + 1) * pcz]
            raw_send[b, j, :, rb:] = sumsq[j * pcz:(j + 1) * pcz]
        for o in range(1, nz):
            d = zp(o)
            remote(raw_send.at[b, d], raw_recv.at[b, mz], rs.at[b, o - 1], rr.at[b, mz], {"feat": d}).start()
        return carry

    lax.fori_loop(0, nb, score_block, 0)

    labels = mz * pcz + lax.broadcasted_iota(jnp.int32, (pcz, rb), 0)
    scores = []
    for b in range(nb):
        acc = raw_send[b, mz]
        for o in range(1, nz):
            s = zp(o)
            wait_recv(raw_recv.at[b, s], rr.at[b, s], {"feat": s})
            acc = acc + raw_recv[b, s]
        scale = 2.5 / math.sqrt(k_total) * lax.rsqrt(acc[:, rb:rb + 1] / k_total + 1e-06)
        owned = owner[:, b * rb:(b + 1) * rb] == labels
        scores.append((owned, acc[:, :rb] * scale))
    top = functools.reduce(jnp.maximum, [
        jnp.max(jnp.where(owned, F32(-1e30), s), axis=1, keepdims=True) for owned, s in scores])
    total = jnp.zeros((pcz, 1), F32)
    for b in range(nb):
        owned, s = scores[b]
        w = jnp.where(owned, F32(0.0), jnp.exp(s - top))
        total = total + jnp.sum(w, axis=1, keepdims=True)
        w_all[mz, :, b * rb:(b + 1) * rb] = w.astype(BF16)
    wz = [remote(w_all.at[mz], w_all.at[mz], ws.at[o - 1], wr.at[mz], {"feat": zp(o)}) for o in range(1, nz)]
    for c in wz:
        c.start()

    full = jnp.zeros((pcz, 128), F32)
    st_x[mx, 0] = top + full
    st_x[mx, 1] = total + full
    sx = [remote(st_x.at[mx], st_x.at[mx], sxs.at[o - 1], sxr.at[mx], {"rows": xp(o)}) for o in range(1, nx)]
    for c in sx:
        c.start()
    for o in range(1, nx):
        s = xp(o)
        wait_recv(st_x.at[s], sxr.at[s], {"rows": s})
    top_x = functools.reduce(jnp.maximum, [st_x[x, 0] for x in range(nx)])
    tot_x = functools.reduce(jnp.add, [jnp.exp(st_x[x, 0] - top_x) * st_x[x, 1] for x in range(nx)])
    st_s[ms, 0] = top_x
    st_s[ms, 1] = tot_x
    ss = remote(st_s.at[ms], st_s.at[ms], sss.at[0], ssr.at[0], {"sub": os})
    ss.start()
    wait_recv(st_s.at[os], ssr.at[0], {"sub": os})
    top_all = functools.reduce(jnp.maximum, [st_s[s, 0] for s in range(ns)])
    tot_all = functools.reduce(jnp.add, [jnp.exp(st_s[s, 0] - top_all) * st_s[s, 1] for s in range(ns)])
    fac[mz] = jnp.exp(st_x[mx, 0] - top_all) / tot_all
    fz = [remote(fac.at[mz], fac.at[mz], fs.at[o - 1], fr.at[mz], {"feat": zp(o)}) for o in range(1, nz)]
    for c in fz:
        c.start()
    for o in range(1, nz):
        s = zp(o)
        wait_recv(w_all.at[s], wr.at[s], {"feat": s})
    for o in range(1, nz):
        s = zp(o)
        wait_recv(fac.at[s], fr.at[s], {"feat": s})

    w_full = w_all[...].reshape(passages, rows)
    factor = fac[...].reshape(passages, 128)[:, :1]

    def sub_copy(b):
        return remote(dbuf.at[b, os], dpart.at[b], d1s.at[b], d1r.at[b], {"sub": os})

    def weighted(b, carry):
        at = pl.ds(pl.multiple_of(b * cb, cb), cb)
        part = jnp.dot(w_full, cor_v[:, at], preferred_element_type=F32) * factor
        part = part.astype(BF16)
        for x in range(nx):
            for s in range(ns):
                i = x * ns + s
                dbuf[b, s, x * pci:(x + 1) * pci, :] = part[i * pci:(i + 1) * pci]
        sub_copy(b).start()
        return carry

    def row_copy(b, o):
        return remote(d2.at[b, xp(o)], d3.at[b, mx], d2s.at[b, o - 1], d2r.at[b, mx], {"rows": xp(o)})

    def merge(b, carry):
        sub_copy(b).wait_recv()
        both = dbuf[b, ms].astype(F32) + dpart[b].astype(F32)
        for x in range(nx):
            d2[b, x] = both[x * pci:(x + 1) * pci].astype(BF16)
        for o in range(1, nx):
            row_copy(b, o).start()
        return carry

    weighted(0, 0)

    def step(b, carry):
        weighted(b, carry)
        return merge(b - 1, carry)

    lax.fori_loop(1, ncb, step, 0)
    merge(ncb - 1, 0)

    def finish(b, carry):
        acc = d2[b, mx].astype(F32)
        for o in range(1, nx):
            s = xp(o)
            wait_recv(d3.at[b, s], d2r.at[b, s], {"rows": s})
            acc = acc + d3[b, s].astype(F32)
        out[:, pl.ds(pl.multiple_of(b * cb, cb), cb)] = acc
        sub_copy(b).wait_send()
        for o in range(1, nx):
            row_copy(b, o).wait_send()
        for o in range(1, nz):
            pass
        return carry

    lax.fori_loop(0, ncb, finish, 0)

    for c in g_copies + x_copies + gi + xz + xi + fw + wz + sx + [ss] + fz:
        c.wait_send()
    for b in range(nb):
        for o in range(1, nz):
            remote(raw_send.at[b, zp(o)], raw_recv.at[b, mz], rs.at[b, o - 1], rr.at[b, mz],
                   {"feat": zp(o)}).wait_send()


def local(activations, out_grads, proj_in, proj_out, lengths, corpus, owner):
    nz, nx, ns = lax.axis_size("feat"), lax.axis_size("rows"), lax.axis_size("sub")
    tok, din = activations.shape
    dout = out_grads.shape[1]
    rank = proj_in.shape[1]
    passages = lengths.shape[0]
    rows, kc = corpus.shape
    cols = rank // nz
    ni = nx * ns
    pcz, pci, tc = passages // nz, passages // ni, tok // nz
    ends = jnp.cumsum(lengths)
    starts = ends - lengths
    base = jnp.minimum(starts // 128 * 128, tok * ni - WINDOW)
    win = jnp.stack([base // 128, starts - base, ends - base, base // 128 + 1])
    nb = 4
    rb = rows // nb
    cb = min(kc, 512)
    ncb = kc // cb
    V, D = pltpu.VMEM, pltpu.SemaphoreType.DMA
    scratch = [
        V((tok, din), BF16), V((tok, dout), BF16), V((din, rank), BF16), V((dout, rank), BF16),
        V((rows, kc), BF16),
        V((nz, cols, tok), F32), V((nz, cols, tok), F32),
        V((nz, tc, rank), F32), V((nz, tc, rank), F32),
        V((tok * ni, rank), BF16), V((cols, tok * ni), BF16),
        V((tok * ni // 128, 128, rank), BF16), V((tok * ni // 128, cols, 128), F32),
        V((cols * passages, rank), F32), V((passages, cols * rank), BF16), V((passages, rank), F32),
        V((nb, nz, pcz, rb + 128), F32), V((nb, nz, pcz, rb + 128), F32),
        V((nz, pcz, rows), BF16),
        V((nx, 2, pcz, 128), F32), V((ns, 2, pcz, 128), F32), V((nz, pcz, 128), F32),
        V((ncb, ns, nx * pci, cb), BF16), V((ncb, nx * pci, cb), BF16),
        V((ncb, nx, pci, cb), BF16), V((ncb, nx, pci, cb), BF16),
        D((nz + 3,)), D((nb,)),
        D((nz,)), D((nz,)), D((nz,)), D((nz,)), D((nz,)), D((nz,)),
        D((nx,)), D((nx,)), D((nx,)), D((nx,)), D((2, nx)), D((2, nx)),
        D((nb, nz)), D((nb, nz)), D((nz,)), D((nz,)), D((nz,)), D((nz,)),
        D((nx,)), D((nx,)), D((1,)), D((1,)),
        D((ncb,)), D((ncb,)), D((ncb, nx)), D((ncb, nx)),
    ]
    anyspace = pl.BlockSpec(memory_space=pl.ANY)
    vmem = pl.BlockSpec(memory_space=pltpu.VMEM)
    return pl.pallas_call(
        functools.partial(kernel, nz, nx, ns),
        out_shape=jax.ShapeDtypeStruct((pci, kc), F32),
        in_specs=[pl.BlockSpec(memory_space=pltpu.SMEM), anyspace, anyspace, anyspace, anyspace, vmem, anyspace],
        out_specs=vmem,
        scratch_shapes=scratch,
        compiler_params=pltpu.CompilerParams(
            collective_id=0, has_side_effects=True, vmem_limit_bytes=67043328),
    )(win, activations, out_grads, proj_in, proj_out, owner.reshape(1, rows), corpus)


def solution(mesh):
    return jax.shard_map(
        local,
        mesh=mesh,
        in_specs=(
            P(("groups", "rows", "sub"), "feat"),
            P(("groups", "rows", "sub"), "feat"),
            P(("groups", "feat"), None),
            P(("groups", "feat"), None),
            P("groups"),
            P(("groups", "rows", "sub"), "feat"),
            P(("rows", "sub")),
        ),
        out_specs=P(("groups", "rows", "sub"), "feat"),
        check_vma=False,
    )
```
